32 devices in a mesh: rows: 8 (over y, x, core), cols: 4 (over z).
Axes of the slice: x: 2, y: 2, z: 4, core: 2. Of those that a mesh axis runs over, the one named last changes fastest.
Arguments:
- tokens: bfloat16 [32768, 768], P(('rows', 'cols')), may hold values from -6 to 6
- cotangent: bfloat16 [32768, 768], P(('rows', 'cols')), may hold values from -6 to 6
- lengths: int32 [32], P('rows'), may hold values from 256 to 1024, as said below
- norm_gain: bfloat16 [768], P('cols'), may hold values from 0.5 to 1.5
- proj_gate: bfloat16 [768, 1536], P('rows', 'cols'), may hold values from -0.21875 to 0.21875
- proj_input: bfloat16 [768, 1536], P('rows', 'cols'), may hold values from -0.21875 to 0.21875
- proj_state: bfloat16 [768, 256], P('rows', 'cols'), may hold values from -0.21875 to 0.21875
- proj_step: bfloat16 [768, 24], P('rows', 'cols'), may hold values from -0.21875 to 0.21875
- conv_taps_x: bfloat16 [4, 1536], P(None, 'cols'), may hold values from -3 to 3
- conv_bias_x: bfloat16 [1536], P('cols'), may hold values from -3 to 3
- conv_taps_bc: bfloat16 [4, 256], P(None, 'cols'), may hold values from -3 to 3
- conv_bias_bc: bfloat16 [256], P('cols'), may hold values from -3 to 3
- step_bias: bfloat16 [24], P('cols'), may hold values from -4 to -1
- decay_log: bfloat16 [24], P('cols'), may hold values from -3 to 1.5
- skip_gain: bfloat16 [24], P('cols'), may hold values from 0.5 to 1.5
- gated_gain: bfloat16 [1536], P('cols'), may hold values from 0.5 to 1.5
- proj_out: bfloat16 [1536, 768], P('cols', 'rows'), may hold values from -0.15625 to 0.15625
Outputs:
- layer_out: bfloat16 [32768, 768], P(('rows', 'cols'))
- grad_tokens: bfloat16 [32768, 768], P(('rows', 'cols'))
- grad_norm_gain: float32 [768], P('cols')
- grad_proj_gate: float32 [768, 1536], P('rows', 'cols')
- grad_proj_input: float32 [768, 1536], P('rows', 'cols')
- grad_proj_state: float32 [768, 256], P('rows', 'cols')
- grad_proj_step: float32 [768, 24], P('rows', 'cols')
- grad_conv_taps_x: float32 [4, 1536], P(None, 'cols')
- grad_conv_bias_x: float32 [1536], P('cols')
- grad_conv_taps_bc: float32 [4, 256], P(None, 'cols')
- grad_conv_bias_bc: float32 [256], P('cols')
- grad_step_bias: float32 [24], P('cols')
- grad_decay_log: float32 [24], P('cols')
- grad_skip_gain: float32 [24], P('cols')
- grad_gated_gain: float32 [1536], P('cols')
- grad_proj_out: float32 [1536, 768], P('cols', 'rows')
The draws below stay inside these ranges and needn't reach their ends.
Inputs may be any that keep to these rules, and one draw needn't show every extreme that they name: `lengths`: entry s is the number of tokens of the sequence in slot s, which fills that slot's first positions; some slot holds 1024 tokens and some slot 256.
All inputs are finite; a program needn't handle non-finite values.
Results may differ from the reference program's by a relative error of at most 0.0093.
Values may be sent and summed in bfloat16 or wider, within the bound.
No kernel may reach another device: no remote copies, remote signals or barrier semaphores. Data moves between devices by JAX's collectives and lax.ppermute only.
A program may use at most 256 MiB of HBM per device.

```python
import math
import jax
import jax.numpy as jnp
from jax import lax

D = 768
H = 24
P_SIZE = 64
N = 128
TAPS = 4
BLOCK = 256
SLOT = 1024
MIN_LEN = 256
SLOTS = 32
TOKENS = 32768


def draw_lengths(key, part):
    first_key = jax.random.fold_in(key, 11)
    second_key = jax.random.fold_in(key, 23)
    third_key = jax.random.fold_in(key, 37)
    drawn = jax.random.randint(first_key, (SLOTS,), MIN_LEN, SLOT + 1, dtype=jnp.int32)
    longest = jax.random.randint(second_key, (), 0, SLOTS, dtype=jnp.int32)
    step_away = jax.random.randint(third_key, (), 1, SLOTS, dtype=jnp.int32)
    shortest = (longest + step_away) % SLOTS
    places = jnp.arange(SLOTS, dtype=jnp.int32)
    drawn = jnp.where(places == longest, SLOT, drawn)
    drawn = jnp.where(places == shortest, MIN_LEN, drawn)
    return drawn.astype(jnp.int32)


def steps_of(key, extent, pieces, low, top_value):
    def one(dim, shards_of):
        draws = jax.random.uniform(jax.random.fold_in(jax.random.fold_in(key, 6), dim), (shards_of,), jnp.float32, low / len(pieces), top_value / len(pieces))
        return jnp.repeat(jnp.exp(draws), extent[dim] // shards_of).reshape((-1,) + (1,) * (len(extent) - dim - 1))

    gain = one(*pieces[0])
    for cut in pieces[1:]:
        gain = gain * one(*cut)
    return gain


def bell_draw(own_key, dims, width, limit, shards=(), held_as=jnp.bfloat16):
    factor_of = steps_of(own_key, dims, shards, -0.22, 0.18) if shards else 1.0
    values = jax.random.normal(own_key, dims, jnp.float32) * width * factor_of
    return jnp.minimum(jnp.maximum(values, -limit), limit).astype(held_as)


def setup_inputs(seed: int = 0) -> dict:
    key_list = jax.random.split(jax.random.key(seed), 18)
    tokens = bell_draw(key_list[0], (TOKENS, D), 1.0, 6.0, ((0, 32),))
    cotangent = bell_draw(key_list[1], (TOKENS, D), 1.0, 6.0, ((0, 32),))
    lengths = draw_lengths(jax.random.fold_in(key_list[17], 71), 0)
    norm_gain = jnp.clip(1.0 + 0.1 * jax.random.normal(key_list[3], (D,), jnp.float32), 0.5, 1.5).astype(jnp.bfloat16)
    proj_gate = bell_draw(key_list[4], (D, H * P_SIZE), D ** -0.5, 0.21875, ((0, 8), (1, 4)))
    proj_input = bell_draw(key_list[5], (D, H * P_SIZE), D ** -0.5, 0.21875, ((0, 8), (1, 4)))
    proj_state = bell_draw(key_list[6], (D, 2 * N), D ** -0.5, 0.21875, ((0, 8), (1, 4)))
    proj_step = bell_draw(key_list[7], (D, H), D ** -0.5, 0.21875, ((0, 8), (1, 4)))
    conv_taps_x = bell_draw(key_list[8], (TAPS, H * P_SIZE), TAPS ** -0.5, 3.0, ((1, 4),))
    conv_bias_x = bell_draw(key_list[9], (H * P_SIZE,), 0.5, 3.0, ((0, 4),))
    conv_taps_bc = bell_draw(key_list[10], (TAPS, 2 * N), TAPS ** -0.5, 3.0, ((1, 4),))
    conv_bias_bc = bell_draw(key_list[11], (2 * N,), 0.5, 3.0, ((0, 4),))
    step_bias = jnp.clip(-4.0 + 3.0 * jax.random.uniform(key_list[12], (H,), jnp.float32) ** steps_of(key_list[12], (H,), ((0, 4),), -0.2, 0.2), -4.0, -1.0).astype(jnp.bfloat16)
    decay_log = jnp.clip(-3.0 + 4.5 * jax.random.uniform(key_list[13], (H,), jnp.float32) ** steps_of(key_list[13], (H,), ((0, 4),), -0.2, 0.2), -3.0, 1.5).astype(jnp.bfloat16)
    skip_gain = jnp.clip(0.5 + 1.0 * jax.random.uniform(key_list[14], (H,), jnp.float32) ** steps_of(key_list[14], (H,), ((0, 4),), -0.2, 0.2), 0.5, 1.5).astype(jnp.bfloat16)
    gated_gain = jnp.clip(1.0 + 0.1 * jax.random.normal(key_list[15], (H * P_SIZE,), jnp.float32), 0.5, 1.5).astype(jnp.bfloat16)
    proj_out = bell_draw(key_list[16], (H * P_SIZE, D), (H * P_SIZE) ** -0.5, 0.15625, ((0, 4), (1, 8)))
    return dict(tokens=tokens, cotangent=cotangent, lengths=lengths, norm_gain=norm_gain, proj_gate=proj_gate, proj_input=proj_input, proj_state=proj_state, proj_step=proj_step, conv_taps_x=conv_taps_x, conv_bias_x=conv_bias_x, conv_taps_bc=conv_taps_bc, conv_bias_bc=conv_bias_bc, step_bias=step_bias, decay_log=decay_log, skip_gain=skip_gain, gated_gain=gated_gain, proj_out=proj_out)


EPSILON = 1e-05
HIGHEST = lax.Precision.HIGHEST

@jax.custom_vjp
def low(v):
    return lax.optimization_barrier(v.astype(jnp.bfloat16)).astype(jnp.float32)

@jax.custom_vjp
def low_back(v):
    return v

def low_keep(v):
    return (low(v), None)

def low_pass(kept, grad):
    return (grad,)

def back_keep(v):
    return (v, None)

def back_low(kept, grad):
    return (low(grad),)
low.defvjp(low_keep, low_pass)
low_back.defvjp(back_keep, back_low)

def block_step(decay_rates, carry_state, block_data):
    inputs, step_sizes, b_rows, c_rows = block_data
    cumulative = jnp.cumsum(step_sizes * decay_rates, axis=1)
    cumulative_heads = jnp.swapaxes(cumulative, 1, 2)
    steps_heads = jnp.swapaxes(step_sizes, 1, 2)
    positions = jnp.arange(inputs.shape[1])
    causal = positions[:, None] >= positions[None, :]
    spacing = cumulative_heads[:, :, :, None] - cumulative_heads[:, :, None, :]
    fading = jnp.where(causal, jnp.exp(jnp.where(causal, spacing, 0.0)), 0.0)
    intersection = jnp.einsum('stn,skn->stk', c_rows, b_rows, precision=HIGHEST)
    mixing = fading * intersection[:, None, :, :] * steps_heads[:, :, None, :]
    inside = jnp.einsum('shtk,skhp->sthp', mixing, inputs, precision=HIGHEST)
    carried = jnp.einsum('stn,shpn->sthp', c_rows, carry_state, precision=HIGHEST) * jnp.exp(cumulative)[..., None]
    remaining = jnp.exp(cumulative[:, -1:, :] - cumulative) * step_sizes
    weighted = inputs * remaining[..., None]
    fresh_part = jnp.einsum('skn,skhp->shpn', b_rows, weighted, precision=HIGHEST)
    updated = carry_state * jnp.exp(cumulative[:, -1, :])[:, :, None, None] + fresh_part
    return (updated, inside + carried)

def state_scan(inputs, step_sizes, decay_rates, b_rows, c_rows):
    batch_size, length, head_count, head_width = inputs.shape
    block_count = length // BLOCK

    def cut_blocks(array_in):
        shaped = array_in.reshape((batch_size, block_count, BLOCK) + array_in.shape[2:])
        return jnp.moveaxis(shaped, 1, 0)
    start_state = jnp.zeros((batch_size, head_count, head_width, b_rows.shape[-1]), jnp.float32)
    walker = jax.checkpoint(block_step)

    def block_walk(carry_state, block_data):
        return walker(decay_rates, carry_state, block_data)
    _, outputs = lax.scan(block_walk, start_state, (cut_blocks(inputs), cut_blocks(step_sizes), cut_blocks(b_rows), cut_blocks(c_rows)))
    return jnp.moveaxis(outputs, 0, 1).reshape(inputs.shape)

def causal_conv(values, tap_weights, offset):
    tap_count = tap_weights.shape[0]
    padded = jnp.pad(values, ((0, 0), (tap_count - 1, 0), (0, 0)))
    length = values.shape[1]
    running = offset + tap_weights[0] * padded[:, 0:length, :]
    for tap_place in range(1, tap_count):
        running = running + tap_weights[tap_place] * padded[:, tap_place:tap_place + length, :]
    return running

def mixer(main_raw, state_raw, step_raw, taps_x, bias_x, taps_bc, bias_bc, step_bias, decay_log, skip_gain):
    head_count = step_raw.shape[-1]
    mixed_x = jax.nn.silu(causal_conv(main_raw, taps_x, bias_x))
    mixed_bc = jax.nn.silu(causal_conv(state_raw, taps_bc, bias_bc))
    half_width = mixed_bc.shape[-1] // 2
    b_rows = mixed_bc[..., :half_width]
    c_rows = mixed_bc[..., half_width:]
    step_sizes = jax.nn.softplus(step_raw + step_bias)
    decay_rates = -jnp.exp(decay_log)
    shaped = mixed_x.reshape(mixed_x.shape[:2] + (head_count, -1))
    scanned = state_scan(shaped, step_sizes, decay_rates, b_rows, c_rows) + skip_gain[:, None] * shaped
    return scanned.reshape(mixed_x.shape)

def group_forward(weights, block_data):
    norm_gain, proj_gate, proj_input, proj_state, proj_step, conv_taps_x, conv_bias_x, conv_taps_bc, conv_bias_bc, step_bias, decay_log, skip_gain, gated_gain, proj_out = weights
    values, live_rows = block_data
    scaled = values * lax.rsqrt(lax.optimization_barrier(jnp.mean(values * values, axis=-1, keepdims=True)) + EPSILON)
    normed = low(scaled * norm_gain)
    gate_pre = low_back(jnp.einsum('std,de->ste', normed, proj_gate, precision=HIGHEST))
    main_raw = low_back(jnp.einsum('std,de->ste', normed, proj_input, precision=HIGHEST))
    state_raw = low_back(jnp.einsum('std,de->ste', normed, proj_state, precision=HIGHEST))
    step_raw = low_back(jnp.einsum('std,de->ste', normed, proj_step, precision=HIGHEST))
    scanned = mixer(main_raw, state_raw, step_raw, conv_taps_x, conv_bias_x, conv_taps_bc, conv_bias_bc, step_bias, decay_log, skip_gain)
    gated_rows = scanned * jax.nn.silu(gate_pre)
    gated_hat = gated_rows * lax.rsqrt(lax.optimization_barrier(jnp.mean(gated_rows * gated_rows, axis=-1, keepdims=True)) + EPSILON)
    result = low(gated_hat * gated_gain)
    branch = jnp.einsum('ste,ed->std', result, proj_out, precision=HIGHEST)
    return live_rows[..., None] * (values + branch)

def reference(tokens, cotangent, lengths, norm_gain, proj_gate, proj_input, proj_state, proj_step, conv_taps_x, conv_bias_x, conv_taps_bc, conv_bias_bc, step_bias, decay_log, skip_gain, gated_gain, proj_out):
    slot_count = lengths.shape[0]
    group_size = math.gcd(slot_count, max(1, 4096 // SLOT))
    positions = jnp.arange(SLOT, dtype=jnp.int32)
    live_mask = (positions[None, :] < lengths[:, None]).astype(jnp.float32)
    block_shape = (slot_count // group_size, group_size, SLOT, tokens.shape[1])
    values = tokens.astype(jnp.float32).reshape(block_shape)
    live_rows = live_mask.reshape(block_shape[:3])
    weights = tuple((weight_item.astype(jnp.float32) for weight_item in (norm_gain, proj_gate, proj_input, proj_state, proj_step, conv_taps_x, conv_bias_x, conv_taps_bc, conv_bias_bc, step_bias, decay_log, skip_gain, gated_gain, proj_out)))

    def forward(values_in, weights_in):
        walker = jax.checkpoint(group_forward)

        def visit_group(block_data):
            return walker(weights_in, block_data)
        return lax.map(visit_group, (values_in, live_rows))
    outputs, pull_back = jax.vjp(forward, values, weights)
    grad_values, grad_weights = pull_back(cotangent.astype(jnp.float32).reshape(block_shape))
    return (outputs.reshape(tokens.shape).astype(jnp.bfloat16), grad_values.reshape(tokens.shape).astype(jnp.bfloat16), grad_weights[0], grad_weights[1], grad_weights[2], grad_weights[3], grad_weights[4], grad_weights[5], grad_weights[6], grad_weights[7], grad_weights[8], grad_weights[9], grad_weights[10], grad_weights[11], grad_weights[12], grad_weights[13])
```

```python
import functools
import jax
import jax.numpy as jnp
from jax import lax
from jax.sharding import PartitionSpec as P
from jax.experimental import pallas as pl
from jax.experimental.pallas import tpu as pltpu

D = 768
H = 24
PW = 64
N = 128
E = H * PW
TAPS = 4
SLOT = 1024
Q = 128
BLK = 256
GBLK = 256
EPSILON = 1e-05
F32 = jnp.float32
BF = jnp.bfloat16
HIGHEST = lax.Precision.HIGHEST
NEG = -1e30
ZB = 4
RB = 8
HB = E // ZB
PR = D // RB
W1 = HB + N
HALF = W1 // 2
FORWARD_PARTS = 2
VMEM_MIB = dict(mixer_forward=13, gating=22, mixer_backward=17, late_gradients=9, input_gradient=12)
BACKWARD_PARTS = 4
SR = 16
BCB = 2 * N // ZB
HPB = H // ZB


def nn(a, b):
    return lax.dot_general(a, b, (((1,), (0,)), ((), ())), preferred_element_type=F32)


def nt(a, b):
    return lax.dot_general(a, b, (((1,), (1,)), ((), ())), preferred_element_type=F32)


def sigmoid(v):
    return 0.5 * jnp.tanh(0.5 * v) + 0.5


def softplus(v):
    return jnp.maximum(v, 0.0) + jnp.log1p(jnp.exp(-jnp.abs(v)))


def fill_spread(spread):
    head = lax.broadcasted_iota(jnp.int32, (2 * N, E), 0) % N
    lane = lax.broadcasted_iota(jnp.int32, (2 * N, E), 1) // PW
    spread[...] = (head == lane).astype(F32).astype(BF)


def hi_lo(v):
    hi = v.astype(BF)
    lo = (v - hi.astype(F32)).astype(BF)
    return hi, lo


def widen(v, spread):
    hi, lo = hi_lo(v)
    return nn(jnp.concatenate([hi, lo], axis=1), spread)


def tri_lower():
    row = lax.broadcasted_iota(jnp.int32, (Q, Q), 0)
    col = lax.broadcasted_iota(jnp.int32, (Q, Q), 1)
    return row, col


def head_steps(step_pre, heads):
    lane = lax.broadcasted_iota(jnp.int32, (1, N), 1)
    rates = jnp.where(lane < H, -jnp.exp(heads[1:2, :]), 0.0)
    dt = softplus(step_pre)
    return dt, rates


def cumulate(dt, rates):
    row, col = tri_lower()
    lower = jnp.where(row >= col, 1.0, 0.0)
    return lax.dot_general(
        lower, dt * rates, (((1,), (0,)), ((), ())), precision=HIGHEST, preferred_element_type=F32
    )


def pair_blocks(pair):
    lane = lax.broadcasted_iota(jnp.int32, (Q, 2 * PW), 1)
    zero = jnp.zeros_like(pair)
    return jnp.concatenate(
        [jnp.where(lane < PW, pair, zero), jnp.where(lane >= PW, pair, zero)], axis=0
    )


def weave_map(transposed):
    shape = (3 * N, ZB * N) if transposed else (ZB * N, 3 * N)
    src = lax.broadcasted_iota(jnp.int32, shape, 1 if transposed else 0)
    dst = lax.broadcasted_iota(jnp.int32, shape, 0 if transposed else 1)
    block, lane = src // N, src % N
    state = (lane < BCB) & (dst == block * BCB + lane)
    step = (lane >= BCB) & (lane < BCB + HPB) & (dst == 2 * N + block * HPB + lane - BCB)
    return (state | step).astype(F32).astype(BF)


def unpack_small(small, chan, chan_bc, heads, gain, spread):
    chan[...] = jnp.zeros_like(chan)
    chan_bc[...] = jnp.zeros_like(chan_bc)
    heads[...] = jnp.zeros_like(heads)
    rows = [small[z].astype(F32) for z in range(ZB)]
    for z in range(ZB):
        lanes = slice(z * HB, (z + 1) * HB)
        chan[0:5, lanes] = rows[z][0:5, :HB]
        chan[6:7, lanes] = rows[z][5:6, :HB]
    for k in range(5):
        chan_bc[k : k + 1, :] = jnp.concatenate(
            [r[6:7, k * BCB : (k + 1) * BCB] for r in rows], axis=1
        )
    for k in range(3):
        at = 5 * BCB + k * HPB
        parts = [r[6:7, at : at + HPB] for r in rows] + [jnp.zeros((1, N - H), F32)]
        heads[k : k + 1, :] = jnp.concatenate(parts, axis=1)
    gain[...] = jnp.zeros_like(gain)
    gain[0:1, :] = jnp.concatenate([r[7:8, : D // ZB] for r in rows], axis=1)
    skip = widen(jnp.broadcast_to(heads[2:3, :], (8, N)), spread[...])
    chan[5:6, :] = skip[0:1, :]


def forward_kernel(first, last, idx, *refs):
    tokens, refs = refs[0], refs[1:]
    if first:
        pieces, refs = refs[:RB], refs[RB:]
    else:
        w1, w_ss, chan, chan_bc, heads, gain, state_i, xhalo_i, bchalo_i = refs[:9]
        refs = refs[9:]
    normed_o, normed_t_o, raw_o, pre_o, bc_raw_o, bc_pre_o, step_o, state_o, scanned_o = refs[:9]
    refs = refs[9:]
    if first:
        w1, w_ss, chan, chan_bc, heads, gain = refs[:6]
        refs = refs[6:]
    if not last:
        state_c, xhalo_c, bchalo_c = refs[:3]
        refs = refs[3:]
    token, refs = refs[0], refs[1:]
    token[...] = jnp.zeros_like(token)
    xbuf, bcbuf, state, spread = refs[:4]
    refs = refs[4:]
    step = pl.program_id(0)

    @pl.when(step == 0)
    def _():
        fill_spread(spread)
        if first:
            (small,) = refs
            xbuf[0:8, :] = jnp.zeros((8, E), F32)
            bcbuf[0:8, :] = jnp.zeros((8, 2 * N), F32)
            state[...] = jnp.zeros_like(state)

            for array, at, half, rel in piece_order():
                lanes = slice(half * HALF, (half + 1) * HALF)
                row = pl.ds(pl.multiple_of((idx[0] ^ rel) * PR, 32), PR)
                for s in range(ZB):
                    block = lax.rem(idx[1] + (ZB - s), ZB)
                    w1[block, row, lanes] = pieces[array][at + s, 0:PR, :]
                    if rel == 0:
                        small[block, :, lanes] = pieces[array][at + s, PR:, :]
            unpack_small(small, chan, chan_bc, heads, gain, spread)
            w_ss[...] = nn(
                jnp.concatenate([w1[z, :, HB:] for z in range(ZB)], axis=1), weave_map(False)
            ).astype(BF)
        else:
            state[...] = state_i[...]
            xbuf[0:8, :] = xhalo_i[...]
            bcbuf[0:8, :] = bchalo_i[...]

    @pl.when(step > 0)
    def _():
        xbuf[0:8, :] = xbuf[BLK : BLK + 8, :]
        bcbuf[0:8, :] = bcbuf[BLK : BLK + 8, :]

    values = tokens[...].astype(F32)
    inv_root = lax.rsqrt(jnp.mean(values * values, axis=1, keepdims=True) + EPSILON)
    normed = (values * inv_root * gain[0:1, :]).astype(BF)
    base = pl.multiple_of(step * BLK, BLK)
    block = pl.ds(base, BLK)
    normed_o[block, :] = normed
    normed_t_o[:, block] = jnp.transpose(normed)
    for z in range(ZB):
        raw = nn(normed, w1[z, :, :HB])
        raw_o[block, z * HB : (z + 1) * HB] = raw.astype(BF)
        xbuf[8 : 8 + BLK, z * HB : (z + 1) * HB] = raw
    ss = nn(normed, w_ss[...])
    bc_raw = ss[:, : 2 * N]
    bc_raw_o[block, :] = bc_raw.astype(BF)
    bcbuf[8 : 8 + BLK, :] = bc_raw
    step_pre = ss[:, 2 * N :] + heads[0:1, :]
    step_o[block, :] = step_pre
    row, col = tri_lower()
    causal = row >= col

    for sub in range(BLK // Q):
        r0 = sub * Q
        chunk = pl.ds(pl.multiple_of(base + r0, Q), Q)
        pre = chan[4:5, :]
        bcp = chan_bc[4:5, :]
        for k in range(TAPS):
            at = 8 + r0 - (TAPS - 1) + k
            pre = pre + chan[k : k + 1, :] * xbuf[at : at + Q, :]
            bcp = bcp + chan_bc[k : k + 1, :] * bcbuf[at : at + Q, :]
        pre_b = pre
        bcp_b = bcp
        pre_o[chunk, :] = pre_b
        bc_pre_o[chunk, :] = bcp_b
        pre = pre_b.astype(F32)
        bcp = bcp_b.astype(F32)
        x = pre * sigmoid(pre)
        bc = bcp * sigmoid(bcp)
        b_low = bc[:, :N].astype(BF)
        c_low = bc[:, N:].astype(BF)
        b_t = jnp.transpose(bc[:, :N]).astype(BF)
        dt, rates = head_steps(step_pre[r0 : r0 + Q, :], heads)
        cum = cumulate(dt, rates)
        cum_t = jnp.transpose(cum)
        ending = cum[Q - 1 : Q, :]
        dt_x = widen(dt, spread[...])
        grow_x = widen(jnp.exp(cum), spread[...])
        left_x = widen(jnp.exp(ending - cum), spread[...])
        fade_x = widen(jnp.broadcast_to(jnp.exp(ending), (8, N)), spread[...])[0:1, :]
        xdt = x * dt_x
        xdt_low = xdt.astype(BF)
        s_low, s_rest = hi_lo(state[...])
        state_o[step * (BLK // Q) + sub] = s_low
        carried = grow_x * nn(
            jnp.concatenate([c_low, c_low], axis=1), jnp.concatenate([s_low, s_rest], axis=0)
        )
        inter = nt(c_low, b_low)
        for pair in range(H // 2):
            mixes = []
            for h in (2 * pair, 2 * pair + 1):
                gap = cum[:, h : h + 1] - cum_t[h : h + 1, :]
                fade = jnp.exp(jnp.where(causal, gap, NEG))
                mixes.append((fade * inter).astype(BF))
            lanes = slice(pair * 2 * PW, (pair + 1) * 2 * PW)
            y = nn(jnp.concatenate(mixes, axis=1), pair_blocks(xdt_low[:, lanes]))
            y = y + carried[:, lanes] + chan[5:6, lanes] * x[:, lanes]
            scanned_o[chunk, lanes] = y
        state[...] = state[...] * fade_x + nn(b_t, (xdt * left_x).astype(BF))

    if not last:

        @pl.when(step == pl.num_programs(0) - 1)
        def _():
            state_c[...] = state[...]
            xhalo_c[...] = xbuf[BLK : BLK + 8, :]
            bchalo_c[...] = bcbuf[BLK : BLK + 8, :]


def piece_order():
    order = []
    for half, (one, two) in enumerate(((2, 4), (4, 2))):
        for k, rels in enumerate(((0, one), (1, one | 1), (two, one | two), (two | 1, one | two | 1))):
            order += [(4 * half + k, ZB * g, half, rel) for g, rel in enumerate(rels)]
    return order


def full(shape):
    return pl.BlockSpec(shape, lambda i, *_: (0,) * len(shape), pipeline_mode=pl.Buffered(1))


ANY = pl.BlockSpec(memory_space=pl.ANY)


def call(kernel, name, grid, idx, ins, outs, scratch, cost, aliases=None):
    return pl.pallas_call(
        kernel,
        grid_spec=pltpu.PrefetchScalarGridSpec(
            num_scalar_prefetch=1,
            grid=(grid,),
            in_specs=[s for _, s in ins],
            out_specs=[s for _, _, s in outs],
            scratch_shapes=scratch,
        ),
        out_shape=[jax.ShapeDtypeStruct(s, d) for s, d, _ in outs],
        input_output_aliases=aliases or {},
        compiler_params=pltpu.CompilerParams(vmem_limit_bytes=VMEM_MIB[name.rstrip("_0123456789")] << 20),
        cost_estimate=pl.CostEstimate(flops=cost[0], bytes_accessed=cost[1], transcendentals=cost[2]),
        name=name,
    )(idx, *[a for a, _ in ins])


def mixer_forward(idx, tokens, source, part, _):
    T = tokens.shape[0]
    parts = FORWARD_PARTS
    steps = T // BLK // parts
    if part:
        kept, carried = source
    for part in (part,):
        first, last = part == 0, part == parts - 1
        off = part * steps

        def rows(shape, axis=0):
            return pl.BlockSpec(
                shape, lambda i, *_: tuple(i + off if a == axis else 0 for a in range(len(shape)))
            )

        half = T // parts
        shapes = [
            ((half, D), BF), ((D, half), BF), ((half, E), BF), ((half, E), F32), ((half, 2 * N), BF),
            ((half, 2 * N), F32), ((half, N), F32), ((half // Q, N, E), BF), ((half, E), F32),
        ]
        outs = [(s, d, full(s)) for s, d in shapes]
        tables = [
            ((ZB, D, W1), BF), ((D, 3 * N), BF), ((8, E), F32), ((8, 2 * N), F32), ((8, N), F32), ((8, D), F32),
        ]
        carry = [((N, E), F32), ((8, E), F32), ((8, 2 * N), F32)]
        ins = [(tokens, rows((BLK, D)))]
        aliases = {}
        scratch = [
            pltpu.VMEM((BLK + 8, E), F32), pltpu.VMEM((BLK + 8, 2 * N), F32),
            pltpu.VMEM((N, E), F32), pltpu.VMEM((2 * N, E), BF),
        ]
        if first:
            ins += [(p, full(p.shape)) for p in source]
            outs += [(s, d, full(s)) for s, d in tables]
            scratch += [pltpu.VMEM((ZB, SR, W1), BF)]
        else:
            ins += [(a, full(a.shape)) for a in kept + carried]
        if not last:
            outs += [(s, d, full(s)) for s, d in carry]
        outs.append(((1, HB), F32, full((1, HB))))
        cost = (T * D * (E + 3 * N) * 2 // parts + T * E * 1280 // parts, (24 << 20) // parts, T * E * 4 // parts)
        got = call(
            functools.partial(forward_kernel, first, last), f"mixer_forward_{part}", steps, idx, ins, outs,
            scratch, cost, aliases,
        )
        made, token = list(got[:9]), got[-1]
        got = list(got[9:-1])
        if first:
            kept, got = got[:6], got[6:]
        carried = got
    return made, kept, carried, token


def gate_kernel(idx, *refs):
    pieces, refs = refs[:RB], refs[RB:]
    normed, normed_t, scanned_r = refs[0:2], refs[2:4], refs[4:6]
    tokens, cot, chan = refs[6:9]
    layer_o, back_o, gates, w_gate, g_gated, g_gain, ga0, ga1, gb0, gb1 = refs[9:19]
    w_out, results, error_t, tmp = refs[19:]
    for array, at, half, rel in piece_order():
        row = pl.ds(pl.multiple_of((idx[0] ^ rel) * PR, 32), PR)
        for s in range(ZB):
            z = lax.rem(idx[1] + (ZB - s), ZB)
            (w_gate, w_out)[half][z, row, :] = pieces[array][at + s]
    g_gated[...] = jnp.zeros_like(g_gated)
    g_gain[...] = jnp.zeros_like(g_gain)

    half_rows = SLOT // FORWARD_PARTS

    def row_block(part, step, carry):
        own = pl.ds(pl.multiple_of(step * GBLK, GBLK), GBLK)
        at = pl.multiple_of(step * GBLK + part * half_rows, GBLK)
        block = pl.ds(at, GBLK)
        position = lax.broadcasted_iota(jnp.int32, (GBLK, 1), 0) + at
        live = jnp.where(position < idx[2], 1.0, 0.0)
        gain = chan[6:7, :]
        normed_b = normed[part][own, :]
        gate = jnp.concatenate([nn(normed_b, w_gate[z]) for z in range(ZB)], axis=1)
        sig = sigmoid(gate)
        act = gate * sig
        scanned = scanned_r[part][own, :]
        gated = scanned * act
        root = lax.rsqrt(jnp.mean(gated * gated, axis=1, keepdims=True) + EPSILON)
        hat = gated * root
        result = (hat * gain).astype(BF)
        branch = jnp.zeros((GBLK, D), F32)
        error = (live * cot[block, :].astype(F32)).astype(BF)
        error_t[:, block] = jnp.transpose(error)
        backs = []
        for z in range(ZB):
            part = result[:, z * HB : (z + 1) * HB]
            results[z, block, :] = part
            branch = branch + nt(part, w_out[z])
            backs.append(nn(error, w_out[z]))
        layer_o[block, :] = (live * (tokens[block, :].astype(F32) + branch)).astype(BF)
        back = jnp.concatenate(backs, axis=1)
        g_gated[0:1, :] += jnp.sum(back * hat, axis=0, keepdims=True)
        weighted = back * gain
        inner = jnp.mean(weighted * hat, axis=1, keepdims=True)
        d_gated = root * (weighted - hat * inner)
        back_o[block, :] = d_gated * act
        low = (d_gated * scanned * (sig * (1.0 + gate * (1.0 - sig)))).astype(BF)
        for z in range(ZB):
            gates[z, block, :] = low[:, z * HB : (z + 1) * HB]
        return carry

    for part in range(FORWARD_PARTS):
        lax.fori_loop(0, half_rows // GBLK, functools.partial(row_block, part), 0)

    def column_block(s, carry):
        block = lax.rem(idx[1] + s, ZB)
        tmp[...] = nn(jnp.concatenate([t[...] for t in normed_t], axis=1), gates[block])
        g_gain[...] += row_sums(tmp[...] * w_gate[block].astype(F32))
        hand_out(idx, s, tmp, ga0, ga1, False)
        tmp[...] = nn(error_t[...], results[block])
        hand_out(idx, s, tmp, gb0, gb1, True)
        return carry

    lax.fori_loop(0, ZB, column_block, 0)


def row_sums(v):
    hi, lo = hi_lo(v)
    ones = jnp.ones((8, v.shape[1]), BF)
    return nt(ones, hi) + nt(ones, lo)


def hand_out(idx, s, src, near, far, flipped):
    width = src.shape[1]
    for rel in range(RB):
        row = pl.multiple_of((idx[0] ^ rel) * PR, 32)
        dx, dy = (rel >> 1) & 1, rel >> 2
        slot = 2 * dy + dx if flipped else 2 * dx + dy
        (far if rel & 1 else near)[slot, s, 0:PR, :] = src[pl.ds(row, PR), :].astype(BF)


def gating(idx, pieces, normed, normed_t, scanned, tokens, cot, chan):
    T = tokens.shape[0]
    ins = [(a, full(a.shape)) for a in pieces + [*normed, *normed_t, *scanned, tokens, cot, chan]]
    shapes = [((T, D), BF), ((T, E), F32), ((ZB, T, HB), BF), ((ZB, D, HB), BF), ((8, E), F32), ((8, D), F32)]
    shapes += [((4, ZB, PR, HB), BF)] * 4
    outs = [(s, d, full(s)) for s, d in shapes]
    scratch = [
        pltpu.VMEM((ZB, D, HB), BF), pltpu.VMEM((ZB, T, HB), BF), pltpu.VMEM((D, T), BF),
        pltpu.VMEM((D, HB), F32),
    ]
    cost = (2 * T * D * E * 5, 28 << 20, T * E * 2)
    return call(gate_kernel, "gating", 1, idx, ins, outs, scratch, cost)


def backward_kernel(first, last, top, waits, idx, *refs):
    back, pre_r, raw_r, bc_pre_r, bc_raw_r, step_r, state_r, chan, chan_bc, heads = refs[:10]
    refs = refs[10:]
    if not first:
        dstate_i, dx_i, dbc_i, gskip_i, gx_i, gbc_i, gh_i = refs[:7]
        refs = refs[7:]
    refs = refs[waits:]
    late_o, gx, gbc, gh = refs[:4]
    refs = refs[4:]
    if not last:
        dstate_c, dx_c, dbc_c, gskip_c = refs[:4]
        refs = refs[4:]
    dstate, dxbuf, dbcbuf, spread, weave, gskip, blocked = refs
    step = pl.program_id(0)

    @pl.when(step == 0)
    def _():
        weave[...] = jnp.zeros_like(weave)
        fill_spread(spread)
        blocked[...] = weave_map(True)
        if first:
            dxbuf[Q : Q + 8, :] = jnp.zeros((8, E), F32)
            dbcbuf[Q : Q + 8, :] = jnp.zeros((8, 2 * N), F32)
            dstate[...] = jnp.zeros_like(dstate)
            gx[...] = jnp.zeros_like(gx)
            gskip[...] = jnp.zeros_like(gskip)
            gbc[...] = jnp.zeros_like(gbc)
            gh[...] = jnp.zeros_like(gh)
        else:
            dxbuf[Q : Q + 8, :] = dx_i[...]
            dbcbuf[Q : Q + 8, :] = dbc_i[...]
            dstate[...] = dstate_i[...]
            gx[...] = gx_i[...]
            gskip[...] = gskip_i[...]
            gbc[...] = gbc_i[...]
            gh[...] = gh_i[...]

    @pl.when(step > 0)
    def _():
        dxbuf[Q : Q + 8, :] = dxbuf[0:8, :]
        dbcbuf[Q : Q + 8, :] = dbcbuf[0:8, :]

    chunk_at = lax.rem(top - step, SLOT // Q // FORWARD_PARTS)
    chunk = pl.ds(pl.multiple_of(chunk_at * Q, Q), Q)
    late_rows = pl.ds(pl.multiple_of((pl.num_programs(0) - 1 - step) * Q, Q), Q)
    row, col = tri_lower()
    anti = col >= row
    spread_1 = spread[0:N, :]
    pre = pre_r[chunk, :].astype(F32)
    sig = sigmoid(pre)
    x = pre * sig
    bcp = bc_pre_r[chunk, :].astype(F32)
    bc_sig = sigmoid(bcp)
    bc = bcp * bc_sig
    b_low = bc[:, :N].astype(BF)
    c_low = bc[:, N:].astype(BF)
    c_t = jnp.transpose(bc[:, N:]).astype(BF)
    step_pre = step_r[chunk, :]
    dt, rates = head_steps(step_pre, heads)
    cum = cumulate(dt, rates)
    cum_t = jnp.transpose(cum)
    ending = cum[Q - 1 : Q, :]
    dt_x = widen(dt, spread[...])
    grow_x = widen(jnp.exp(cum), spread[...])
    left_x = widen(jnp.exp(ending - cum), spread[...])
    fade_x = widen(jnp.broadcast_to(jnp.exp(ending), (8, N)), spread[...])[0:1, :]
    xdt = x * dt_x
    xdt_low = xdt.astype(BF)
    dy = back[pl.ds(pl.multiple_of((top - step) * Q, Q), Q), :]
    dy_low = dy.astype(BF)
    dy_grow = (dy * grow_x).astype(BF)
    s_low = state_r[chunk_at]
    ds = dstate[...]
    ds_low, ds_rest = hi_lo(ds)
    tail = left_x * nn(
        jnp.concatenate([b_low, b_low], axis=1), jnp.concatenate([ds_low, ds_rest], axis=0)
    )
    inter_t = nt(b_low, c_low)
    d_inter_t = jnp.zeros((Q, Q), F32)
    for pair in range(H // 2):
        lanes = slice(pair * 2 * PW, (pair + 1) * 2 * PW)
        blocks = pair_blocks(dy_low[:, lanes])
        d_mix = nt(xdt_low[:, lanes], blocks)
        mixes = []
        for j, h in enumerate((2 * pair, 2 * pair + 1)):
            gap = cum_t[h : h + 1, :] - cum[:, h : h + 1]
            fade = jnp.exp(jnp.where(anti, gap, NEG))
            mix = (fade * inter_t).astype(BF)
            mixes.append(mix)
            d_mix_h = d_mix[:, j * Q : (j + 1) * Q]
            d_inter_t = d_inter_t + fade * d_mix_h
            weave[h : h + 1, :] = jnp.sum(mix.astype(F32) * d_mix_h, axis=0, keepdims=True)
        d_xdt = nn(jnp.concatenate(mixes, axis=1), blocks)
        dxbuf[0:Q, lanes] = d_xdt + tail[:, lanes]
    d_xdt = dxbuf[0:Q, :]
    xdt_f = xdt_low.astype(F32)
    q1_hi, q1_lo = hi_lo(xdt_f * d_xdt)
    q2_hi = (dy * grow_x * nn(c_low, s_low)).astype(BF)
    q3_hi = (x * d_xdt).astype(BF)
    ends = jnp.sum(xdt_f * tail, axis=0, keepdims=True) + fade_x * jnp.sum(
        ds * s_low.astype(F32), axis=0, keepdims=True
    )
    e_hi, e_lo = hi_lo(jnp.broadcast_to(ends, (16, E)))
    sums = nt(jnp.concatenate([q1_hi, q1_lo, q2_hi, q3_hi, e_hi, e_lo], axis=0), spread_1)
    q1 = sums[0:Q] + sums[Q : 2 * Q]
    q2 = sums[2 * Q : 3 * Q]
    q3 = sums[3 * Q : 4 * Q]
    end = sums[4 * Q : 4 * Q + 1] + sums[4 * Q + 16 : 4 * Q + 17]
    d_cum = jnp.transpose(weave[...]) + q2 - q1
    d_cum = d_cum + jnp.where(row == Q - 1, end, 0.0)
    upper = jnp.where(anti, 1.0, 0.0)
    d_a = lax.dot_general(
        upper, d_cum, (((1,), (0,)), ((), ())), precision=HIGHEST, preferred_element_type=F32
    )
    d_dt = q3 + d_a * rates
    d_step = d_dt * sigmoid(step_pre)
    gh[0:1, :] += jnp.sum(d_step, axis=0, keepdims=True)
    gh[1:2, :] += jnp.sum(d_a * dt, axis=0, keepdims=True) * rates
    d_inter_low = d_inter_t.astype(BF)
    d_inter = jnp.transpose(d_inter_t).astype(BF)
    d_c = nn(d_inter, b_low) + nt(dy_grow, s_low)
    d_b = nn(d_inter_low, c_low) + nt((xdt * left_x).astype(BF), ds_low)
    dstate[...] = ds * fade_x + nn(c_t, dy_grow)
    slope_bc = bc_sig * (1.0 + bcp * (1.0 - bc_sig))
    d_bcp = jnp.concatenate([d_b, d_c], axis=1) * slope_bc
    dbcbuf[0:Q, :] = d_bcp
    gskip[0:1, :] += jnp.sum(dy * x, axis=0, keepdims=True)
    d_pre = (d_xdt * dt_x + chan[5:6, :] * dy) * (sig * (1.0 + pre * (1.0 - sig)))
    dxbuf[0:Q, :] = d_pre
    raw = raw_r[chunk, :].astype(F32)
    bc_raw = bc_raw_r[chunk, :].astype(F32)
    gx[4:5, :] += jnp.sum(d_pre, axis=0, keepdims=True)
    gbc[4:5, :] += jnp.sum(d_bcp, axis=0, keepdims=True)
    d_raw = jnp.zeros((Q, E), F32)
    d_bc = jnp.zeros((Q, 2 * N), F32)
    for j in range(TAPS):
        k = TAPS - 1 - j
        ahead = dxbuf[j : j + Q, :]
        d_raw = d_raw + chan[k : k + 1, :] * ahead
        gx[k : k + 1, :] += jnp.sum(raw * ahead, axis=0, keepdims=True)
        ahead = dbcbuf[j : j + Q, :]
        d_bc = d_bc + chan_bc[k : k + 1, :] * ahead
        gbc[k : k + 1, :] += jnp.sum(bc_raw * ahead, axis=0, keepdims=True)
    ss = jnp.concatenate([d_bc.astype(BF), d_step.astype(BF)], axis=1)
    ss = nn(ss, blocked[...]).astype(BF)
    main = d_raw.astype(BF)
    for z in range(ZB):
        late_o[z, late_rows, 0:HB] = main[:, z * HB : (z + 1) * HB]
        late_o[z, late_rows, HB:] = ss[:, z * N : (z + 1) * N]

    @pl.when(step == pl.num_programs(0) - 1)
    def _():
        if last:
            hi, lo = hi_lo(jnp.broadcast_to(gskip[0:1, :], (16, E)))
            total = nt(hi, spread_1) + nt(lo, spread_1)
            gh[2:3, :] = total[0:1, :]
        else:
            dstate_c[...] = dstate[...]
            dx_c[...] = dxbuf[0:8, :]
            dbc_c[...] = dbcbuf[0:8, :]
            gskip_c[...] = gskip[...]


def mixer_backward(idx, back, saved, kept, part, before, after):
    side = 1 - part * FORWARD_PARTS // BACKWARD_PARTS
    normed, normed_t, raw, pre, bc_raw, bc_pre, step, states, scanned = [a[side] for a in saved]
    w1, w_ss, chan, chan_bc, heads, gain = kept
    T = back.shape[0]
    chunks = T // Q
    parts = BACKWARD_PARTS
    steps = chunks // parts
    if part:
        _, sums, carried = before
    for part in (part,):
        first, last = part == 0, part == parts - 1
        top = chunks - 1 - part * steps

        ins = [
            (a, full(a.shape))
            for a in (back, pre, raw, bc_pre, bc_raw, step, states, chan, chan_bc, heads)
        ]
        if not first:
            ins += [(a, full(a.shape)) for a in carried + sums]
        ins += [(a, ANY) for a in after]
        shapes = [((8, E), F32), ((8, 2 * N), F32), ((8, N), F32)]
        outs = [((ZB, steps * Q, W1), BF, full((ZB, steps * Q, W1)))] + [(s, d, full(s)) for s, d in shapes]
        if not last:
            carry = [((N, E), F32), ((8, E), F32), ((8, 2 * N), F32), ((8, E), F32)]
            outs += [(s, d, full(s)) for s, d in carry]
        scratch = [
            pltpu.VMEM((N, E), F32), pltpu.VMEM((Q + 8, E), F32), pltpu.VMEM((Q + 8, 2 * N), F32),
            pltpu.VMEM((2 * N, E), BF), pltpu.VMEM((N, Q), F32), pltpu.VMEM((8, E), F32),
            pltpu.VMEM((3 * N, ZB * N), BF),
        ]
        cost = (2 * T * E * 2048 // parts, (20 << 20) // parts, T * E * 4 // parts)
        got = call(
            functools.partial(backward_kernel, first, last, top, len(after)), f"mixer_backward_{part}", steps, idx, ins, outs,
            scratch, cost,
        )
        made, sums, carried = got[0], list(got[1:4]), list(got[4:])
    return made, sums, carried


def small_tables(idx, gx, gbc, gh, g_gated, g_gain, small_o):
    for z in range(ZB):
        misc = [gbc[k : k + 1, z * BCB : (z + 1) * BCB] for k in range(5)]
        misc += [gh[k : k + 1, z * HPB : (z + 1) * HPB] for k in range(3)]
        misc.append(jnp.zeros((1, HB - 5 * BCB - 3 * HPB), F32))
        lanes = slice(z * HB, (z + 1) * HB)
        wide = slice(z * (D // ZB), (z + 1) * (D // ZB))
        last = jnp.concatenate([g_gain[0:1, wide], jnp.zeros((1, HB - D // ZB), F32)], axis=1)
        slot = lax.rem(ZB + z - idx[1], ZB)
        small_o[slot] = jnp.concatenate(
            [gx[0:5, lanes], g_gated[0:1, lanes], jnp.concatenate(misc, axis=1), last], axis=0
        )


def input_kernel(idx, *refs):
    late, refs = refs[:BACKWARD_PARTS], refs[BACKWARD_PARTS:]
    gates, w_gate, w1, tokens, cot, gain = refs[:6]
    grad_o, token = refs[-2:]
    token[...] = jnp.zeros_like(token)
    size = SLOT // BACKWARD_PARTS
    for part in range(BACKWARD_PARTS):
        block = slice(part * size, (part + 1) * size)
        position = lax.broadcasted_iota(jnp.int32, (size, 1), 0) + part * size
        live = jnp.where(position < idx[2], 1.0, 0.0)
        back = jnp.zeros((size, D), F32)
        for z in range(ZB):
            back = back + nt(gates[z, block, :], w_gate[z]) + nt(late[part][z], w1[z])
        values = tokens[block, :].astype(F32)
        inv_root = lax.rsqrt(jnp.mean(values * values, axis=1, keepdims=True) + EPSILON)
        scaled = values * inv_root
        back = back * gain[0:1, :]
        inner = jnp.mean(back * scaled, axis=1, keepdims=True)
        grad = live * cot[block, :].astype(F32) + inv_root * (back - scaled * inner)
        grad_o[block, :] = grad.astype(BF)


def input_gradient(idx, gates, late, w_gate, w1, tokens, cot, gain, after):
    T = tokens.shape[0]
    ins = [(a, full(a.shape)) for a in [*late, gates, w_gate, w1, tokens, cot, gain]]
    ins += [(a, ANY) for a in after]
    outs = [((T, D), BF, full((T, D))), ((1, HB), F32, full((1, HB)))]
    cost = (2 * T * D * (2 * E + 512), 20 << 20, T)
    return call(input_kernel, "input_gradient", 1, idx, ins, outs, [], cost)


def late_kernel(
    idx, *refs
):
    normed_t, late = refs[:FORWARD_PARTS], refs[FORWARD_PARTS : FORWARD_PARTS + BACKWARD_PARTS]
    w1, gain, gain_i, gx, gbc, gh, g_gated = refs[FORWARD_PARTS + BACKWARD_PARTS :][:7]
    small_o, a0, a1, b0, b1, tmp, g_gain = refs[-7:]
    step = pl.program_id(0)

    @pl.when(step == 0)
    def _():
        g_gain[...] = gain_i[...]

    block = lax.rem(idx[1] + step, ZB)
    tmp[...] = nn(
        jnp.concatenate([t[...] for t in normed_t], axis=1),
        jnp.concatenate([p[block] for p in late], axis=0),
    )
    g_gain[...] += row_sums(tmp[...] * w1[block].astype(F32))

    @pl.when(step == pl.num_programs(0) - 1)
    def _():
        g_gain[...] = g_gain[...] / gain[0:1, :]
        small_tables(idx, gx, gbc, gh, g_gated, g_gain, small_o)

    hand_out(idx, step, tmp.at[:, 0:HALF], a0, a1, False)
    hand_out(idx, step, tmp.at[:, HALF:], b0, b1, True)


def late_gradients(idx, normed_t, late, w1, gain, gain_part, sums, g_gated, after):
    T = SLOT
    ins = [(a, full(a.shape)) for a in [*normed_t, *late]]
    ins += [(a, full(a.shape)) for a in [w1, gain, gain_part] + sums + [g_gated]]
    ins += [(a, ANY) for a in after]
    outs = [((ZB, 8, HB), F32, full((ZB, 8, HB)))] + [((4, ZB, PR, HALF), BF, full((4, ZB, PR, HALF)))] * 4
    scratch = [pltpu.VMEM((D, W1), F32), pltpu.VMEM((8, D), F32)]
    cost = (2 * T * D * ZB * W1, 12 << 20, 0)
    return call(late_kernel, "late_gradients", ZB, idx, ins, outs, scratch, cost)


def swap(array, bit):
    return lax.ppermute(array, "rows", [(i, i ^ bit) for i in range(RB)])


def gather_columns(piece):
    return [piece] + [
        lax.ppermute(piece, "cols", [(j, (j + s) % ZB) for j in range(ZB)]) for s in range(1, ZB)
    ]


def plain_call(kernel, name, ins, shapes, aliases=None):
    return pl.pallas_call(
        kernel,
        in_specs=[s for _, s in ins],
        out_specs=[ANY if aliases else pl.BlockSpec(memory_space=pltpu.VMEM) for _ in shapes],
        out_shape=[jax.ShapeDtypeStruct(*s) for s in shapes],
        input_output_aliases=aliases or {},
        compiler_params=pltpu.CompilerParams(vmem_limit_bytes=4 << 20),
        cost_estimate=pl.CostEstimate(flops=0, bytes_accessed=1 << 18, transcendentals=0),
        name=name,
    )(*[a for a, _ in ins])


LOCAL = pl.BlockSpec(memory_space=pltpu.VMEM)


def hold(values, after):
    return plain_call(
        lambda *refs: None, "hold", [(v, ANY) for v in values] + [(a, ANY) for a in after],
        [(v.shape, v.dtype) for v in values], {k: k for k in range(len(values))},
    )


def halves_kernel(cut, *refs):
    parts, (low, high) = refs[:ZB], refs[ZB:]
    for s in range(ZB):
        low[s] = parts[s][:, :cut]
        high[s] = parts[s][:, cut:]


def gather_near(parts, cut):
    r, w = parts[0].shape
    own = plain_call(
        functools.partial(halves_kernel, cut), "halves", [(p, LOCAL) for p in parts],
        [((ZB, r, cut), BF), ((ZB, r, w - cut), BF)],
    )
    return [(o, swap(o, bit)) for o, bit in zip(own, (2, 4))]


def join_kernel(waits, a, b, c, d, *refs):
    low, high = refs[waits:]
    low[0:ZB] = a[...]
    low[ZB:] = b[...]
    high[0:ZB] = c[...]
    high[ZB:] = d[...]


def join(halves, after=()):
    flat = [a for h in halves for a in h]
    return plain_call(
        functools.partial(join_kernel, len(after)), "join",
        [(a, LOCAL) for a in flat] + [(a, ANY) for a in after],
        [((2 * ZB,) + h[0].shape[1:], BF) for h in halves],
    )


def pack_kernel(main, state, step, gate, out, t_x, b_x, gated, t_bc, b_bc, s_b, d_l, s_g, gain, first, second):
    hc, bc, hp = main.shape[1], state.shape[0], step.shape[0]
    used = hc + bc + hp
    columns = [jnp.transpose(a[...].astype(F32)).astype(BF) for a in (state, step)]
    first[0:PR, :] = jnp.concatenate([main[...]] + columns + [jnp.zeros((PR, W1 - used), BF)], axis=1)
    misc = [t_bc[k : k + 1, :] for k in range(TAPS)] + [b_bc[...], s_b[...], d_l[...], s_g[...]]
    misc = [m.astype(F32) for m in misc]
    misc.append(jnp.zeros((1, hc - sum(m.shape[1] for m in misc)), F32))
    last = [gain[...].astype(F32), jnp.zeros((1, hc - gain.shape[1]), F32)]
    rows = [t_x[...].astype(F32), b_x[...].astype(F32), gated[...].astype(F32)]
    rows += [jnp.concatenate(misc, axis=1), jnp.concatenate(last, axis=1), jnp.zeros((SR - 8, hc), F32)]
    table = jnp.concatenate(rows, axis=0)
    first[PR:, :] = jnp.concatenate([table, jnp.zeros((SR, W1 - hc), F32)], axis=1).astype(BF)
    second[:, :HB] = gate[...]
    second[:, HB:] = out[...]


def pack(weights, smalls):
    gate, main, state, step, out = weights
    flat = [a if a.ndim == 2 else a[None] for a in smalls]
    arrays = [main, state.T, step.T, gate, out.T] + flat
    shapes = [((PR + SR, W1), BF), ((PR, 2 * HB), BF)]
    return pl.pallas_call(
        pack_kernel,
        grid=(1,),
        in_specs=[full(a.shape) for a in arrays],
        out_specs=[full(s) for s, _ in shapes],
        out_shape=[jax.ShapeDtypeStruct(*s) for s in shapes],
        compiler_params=pltpu.CompilerParams(vmem_limit_bytes=4 << 20),
        name="pack",
    )(*arrays)


def gather_far(halves):
    return [swap(h, bit) for h, bit in zip(halves, (4, 2))]


def gather_core(halves):
    return [swap(h, 1) for h in halves]


def listed(near, near_core, far, far_core):
    return [a[half] for half in range(2) for a in (near, near_core, far, far_core)]


def add(left, right):
    return left.astype(F32) + right.astype(F32)


def reduce_core(a0, a1, b0, b1):
    out = []
    for near, far in ((a0, a1), (b0, b1)):
        got = swap(far, 1)
        out.append((add(near[:2], got[:2]), add(near[2:], got[2:]).astype(BF)))
    return out


def reduce_near(halves):
    out = []
    for (keep, send), bit in zip(halves, (2, 4)):
        got = swap(send, bit)
        out.append((add(keep[0], got[0]), add(keep[1], got[1]).astype(BF)))
    return out


def reduce_far(halves):
    totals = [add(keep, swap(send, bit)) for (keep, send), bit in zip(halves, (4, 2))]
    total = jnp.concatenate(totals, axis=2)
    return total[0], [total[s].astype(BF) for s in range(1, ZB)]


def reduce_columns(total, sends):
    for s, send in enumerate(sends, 1):
        total = add(total, lax.ppermute(send, "cols", [(j, (j + s) % ZB) for j in range(ZB)]))
    return total


def whole_of(got, at, width):
    count = got.shape[1]
    return jnp.transpose(got[:, :, :, at : at + width], (0, 2, 1, 3)).reshape(-1, count * width)


def blocks_of(array, width):
    return jnp.transpose(array.reshape(RB, PR, ZB, width), (0, 2, 1, 3))


def merge(blocks):
    return jnp.transpose(blocks, (0, 2, 1, 3)).reshape(D, -1)


def small_rows(taps_x, bias_x, gated, taps_bc, bias_bc, step_bias, decay, skip, gain):
    width = bias_x.shape[0]
    misc = jnp.concatenate([taps_bc.reshape(-1), bias_bc, step_bias, decay, skip])
    rows = [bias_x, gated, misc, gain]
    rows = [jnp.pad(r, (0, width - r.shape[0]))[None] for r in rows]
    return jnp.concatenate([taps_x] + rows, axis=0)


def unpack_rows(rows, width, bc, hp, gain):
    misc = rows[6]
    at = TAPS * bc
    vectors = [misc[at : at + bc]]
    at += bc
    vectors += [misc[at + k * hp : at + (k + 1) * hp] for k in range(3)]
    return [rows[:TAPS, :width], rows[4, :width], misc[: TAPS * bc].reshape(TAPS, bc)] + vectors + [rows[5, :width], rows[7, :gain]]


def general_gather(R, hc, rows, cols, weights, smalls):
    gate, main, state, step, out = weights
    bc, hp = 2 * N // cols, H // cols
    piece = jnp.concatenate([gate, main, out.T, state, step], axis=1)
    got = lax.all_gather(lax.all_gather(piece, "cols", axis=0), "rows", axis=0)
    w_gate, w_in, w_out = [blocks_of(whole_of(got, k * hc, hc), HB) for k in range(3)]
    w_state = blocks_of(whole_of(got, 3 * hc, bc), BCB)
    w_step = blocks_of(whole_of(got, 3 * hc + bc, hp), HPB)
    pad = jnp.zeros((RB, ZB, PR, N - BCB - HPB), BF)
    first = jnp.concatenate([w_in, w_state, w_step, pad], axis=3)
    full_small = [lax.all_gather(s, "cols", axis=s.ndim - 1, tiled=True) for s in smalls]
    tables = []
    for z in range(ZB):
        cut = []
        for s in full_small:
            w = s.shape[-1] // ZB
            cut.append(s[..., z * w : (z + 1) * w])
        tables.append(jnp.pad(small_rows(*cut), ((0, SR - 8), (0, W1 - HB))))
    tables = jnp.broadcast_to(jnp.stack(tables)[None], (RB, ZB, SR, W1))
    first = jnp.concatenate([first, tables], axis=2)
    first, w_gate, w_out = [
        jnp.concatenate([w[:, (ZB - s) % ZB][:, None] for s in range(ZB)], axis=1)
        for w in (first, w_gate, w_out)
    ]

    def grouped(low, high):
        out = [[] for _ in range(RB)]
        for array, _, half, rel in piece_order():
            out[array].append((low, high)[half][rel])
        return [jnp.concatenate(o, axis=0) for o in out]

    return grouped(first[..., :HALF], first[..., HALF:]), grouped(w_gate, w_out)


def general_reduce(near, far, flipped):
    blocks = []
    for rel in range(RB):
        dx, dy = (rel >> 1) & 1, rel >> 2
        blocks.append((far if rel & 1 else near)[2 * dy + dx if flipped else 2 * dx + dy])
    return jnp.stack(blocks)


def body(
    tokens, cotangent, lengths, norm_gain, proj_gate, proj_input, proj_state, proj_step,
    conv_taps_x, conv_bias_x, conv_taps_bc, conv_bias_bc, step_bias, decay_log, skip_gain,
    gated_gain, proj_out,
):
    R, hc = proj_gate.shape
    rows, cols = D // R, E // hc
    bc, hp = 2 * N // cols, H // cols
    T = tokens.shape[0]
    assert T == SLOT
    direct = (rows, cols) == (RB, ZB)
    i, z = lax.axis_index("rows"), lax.axis_index("cols")
    length = lax.dynamic_slice_in_dim(lengths, z, 1)[0]
    zero = jnp.int32(0)
    idx = jnp.stack([i if direct else zero, z if direct else zero, length]).astype(jnp.int32)
    smalls = (conv_taps_x, conv_bias_x, gated_gain, conv_taps_bc, conv_bias_bc, step_bias, decay_log, skip_gain, norm_gain)
    if direct:
        first, second = pack((proj_gate, proj_input, proj_state, proj_step, proj_out), smalls)
        first, second = gather_columns(first), gather_columns(second)
        first = join(gather_near(first, HALF))
        first_far = hold(gather_far(first), second)
        first = listed(first, gather_core(first), first_far, gather_core(first_far))
        second = gather_near(second, HB)
    else:
        first, second = general_gather(
            R, hc, rows, cols, (proj_gate, proj_input, proj_state, proj_step, proj_out), smalls
        )
    saved, kept, carried, token = mixer_forward(idx, tokens, first, 0, None)
    if direct:
        second = join(second, [token])
        second_far, second_core = gather_far(second), gather_core(second)
    saved_b, _, _, token = mixer_forward(idx, tokens, (kept, carried), 1, None)
    if direct:
        second_far = hold(second_far, [token])
        second = listed(second, second_core, second_far, gather_core(second_far))
    saved = list(zip(saved, saved_b))
    normed, normed_t, scanned = saved[0], saved[1], saved[8]
    layer_out, back, gates, w_gate, g_gated, g_gain, *early = gating(
        idx, second, normed, normed_t, scanned, tokens, cotangent, kept[2]
    )
    made, after, late = (), [], []
    if direct:
        early = reduce_core(*early)
        after = [send for _, send in early]
    for part in range(BACKWARD_PARTS):
        made = mixer_backward(idx, back, saved, kept, part, made, after)
        late.insert(0, made[0])
        if direct and part == 0:
            early = reduce_near(early)
            after = [send for _, send in early]
        elif direct and part == 1:
            early = reduce_far(early)
            after = early[1]
        elif direct and part == 2:
            early = reduce_columns(*early)
            after = []
        elif direct:
            after = [early]
    sums = list(made[1])
    small, *late_parts = late_gradients(idx, normed_t, late, kept[0], kept[5], g_gain, sums, g_gated, after)
    after = []
    if direct:
        late_parts = reduce_core(*late_parts)
        after = [send for _, send in late_parts]
        small = reduce_columns(small[0], [small[s] for s in range(1, ZB)])
    grad_tokens, token = input_gradient(idx, gates, late, w_gate, kept[0], tokens, cotangent, kept[5], after)
    if direct:
        keeps = hold([keep for keep, _ in late_parts], [token])
        late_parts = reduce_near([(keep, send) for keep, (_, send) in zip(keeps, late_parts)])
        (small,) = hold([small], [send for _, send in late_parts])
        for bit in (1, 2, 4):
            small = small + swap(small, bit)
        g_first = reduce_columns(*reduce_far(late_parts))
        g_gate, g_out = early[:, :HB], early[:, HB:]
        g_input, g_state, g_step = g_first[:, :hc], g_first[:, hc : hc + bc], g_first[:, hc + bc : hc + bc + hp]
    else:
        blocks = jnp.concatenate(
            [general_reduce(late_parts[0], late_parts[1], False), general_reduce(late_parts[2], late_parts[3], True)], axis=3
        )
        main = [blocks[..., a:b] for a, b in ((0, HB), (HB, HB + BCB), (HB + BCB, HB + BCB + HPB))]
        grads = [merge(general_reduce(early[0], early[1], False)), merge(general_reduce(early[2], early[3], True))]
        grads += [merge(m) for m in main]
        widths = [hc, hc, hc, bc, hp]
        send = jnp.concatenate(
            [jnp.transpose(g.reshape(rows, R, cols, w), (0, 2, 1, 3)) for g, w in zip(grads, widths)], axis=3
        )
        got = lax.psum_scatter(send, "rows", scatter_dimension=0, tiled=True)
        got = lax.psum_scatter(got, "cols", scatter_dimension=1, tiled=True)[0, 0].astype(F32)
        g_gate, g_out, g_input, g_state, g_step = [
            got[:, sum(widths[:k]) : sum(widths[: k + 1])] for k in range(5)
        ]
        per = [unpack_rows(small[s], HB, BCB, HPB, D // ZB) for s in range(ZB)]
        small = [jnp.concatenate([p[k] for p in per], axis=-1) for k in range(9)]
        small = [
            lax.psum(lax.psum_scatter(s, "cols", scatter_dimension=s.ndim - 1, tiled=True), "rows") for s in small
        ]
    if direct:
        small = unpack_rows(small, hc, bc, hp, D // cols)
    t_x, b_x, t_bc, b_bc, s_b, d_l, s_g, gated, gain = small
    return (
        layer_out, grad_tokens, gain, g_gate, g_input, g_state, g_step, t_x, b_x, t_bc, b_bc, s_b, d_l, s_g,
        gated, g_out.T,
    )


def solution(mesh):
    both = P(("rows", "cols"), None)
    weight, vector, table = P("rows", "cols"), P("cols"), P(None, "cols")
    in_specs = (
        both, both, P("rows"), vector, weight, weight, weight, weight, table, vector, table, vector,
        vector, vector, vector, vector, P("cols", "rows"),
    )
    out_specs = (
        both, both, vector, weight, weight, weight, weight, table, vector, table, vector,
        vector, vector, vector, vector, P("cols", "rows"),
    )
    return jax.shard_map(body, mesh=mesh, in_specs=in_specs, out_specs=out_specs, check_vma=False)
```
